32 devices in a mesh: tm: 8 (over z, x), rows: 4 (over y, core).
Axes of the slice: x: 2, y: 2, z: 4, core: 2. Of those that a mesh axis runs over, the one named last changes fastest.
Arguments:
- sensed_flows_levels: float32 [32, 512], P('tm'), may hold values from -6 to 6
- reading_mask: int32 [32, 512], P('tm'), may hold values 0 or 1
- inventory_propagator: float32 [1024, 1024], replicated, may hold values from -1 to 1
- observation_matrix: float32 [512, 1024], replicated, may hold values from -0.1875 to 0.1875
- measurement_weight: float32 [512], replicated, may hold values from 0.05 to 0.3
- diagonal_blend_factor: float32 [32, 1024], P('tm', 'rows'), may hold values from 0 to 1
- prior_inventory_mean: float32 [1024], replicated, may hold values from -6 to 6
Outputs:
- updated_inventory_means: float32 [32, 1024], P('tm', 'rows')
- reconciled_inventories: float32 [32, 1024], P('tm', 'rows')
The draws below stay inside these ranges and needn't reach their ends.
All inputs are finite; a program needn't handle non-finite values. No bound on the sum of `reading_mask` on one device may be relied on, other than what follows from the above.
Results may differ from the reference program's by a relative error of at most 0.0003.
Values sent between devices are 32-bit elements; how exact they have to be, the bound alone decides.
A program may use at most 64 MiB of HBM per device.

```python
import jax
import jax.numpy as jnp
from jax import lax

N = 1024
MEASURE_COUNT = 512
STEPS_DEV = 4
TOTAL_STEPS = 32


def draw_inventory_propagator(key, part):
    first_key, second_key = jax.random.split(key)
    diagonal = jax.random.uniform(first_key, (N, 1), jnp.float32, 0.994, 0.998)
    limit = 0.002 / N
    mixing = jnp.clip(jax.random.normal(second_key, (N, N), jnp.float32) * (0.5 * limit), -limit, limit)
    row_ids = jax.lax.broadcasted_iota(jnp.int32, (N, N), 0)
    col_ids = jax.lax.broadcasted_iota(jnp.int32, (N, N), 1)
    return jnp.where(row_ids == col_ids, diagonal, mixing)


def draw_diagonal_blend_factor(key, part):
    random_keys = jax.random.split(key, 6)
    slow_share = 4
    slow_flag = jax.random.randint(random_keys[0], (1, N), 0, 8) < slow_share
    slow_rate = 1.4 * jax.random.uniform(random_keys[1], (1, N), jnp.float32, 0.5, 1.0) / TOTAL_STEPS
    fast_rate = 2.302585 / jax.random.uniform(random_keys[2], (1, N), jnp.float32, 30.0, 50.0)
    rate = jnp.where(slow_flag, slow_rate, fast_rate)
    block_factor = jax.random.uniform(random_keys[3], (TOTAL_STEPS // STEPS_DEV, 1, 1), jnp.float32, 0.5, 2.0)
    block_factor = jnp.broadcast_to(block_factor, (TOTAL_STEPS // STEPS_DEV, STEPS_DEV, N)).reshape(TOTAL_STEPS, N)
    gain_vector = jnp.exp(-rate * block_factor)
    surge_flag = jax.random.randint(random_keys[4], (TOTAL_STEPS, 1), 0, TOTAL_STEPS) < 3
    surge_length = jax.random.uniform(random_keys[5], (TOTAL_STEPS, 1), jnp.float32, 0.5, 0.8)
    return gain_vector * jnp.where(surge_flag, surge_length, 1.0)


def touch_ends(result, key, low, largest):
    spot = [jax.random.randint(jax.random.fold_in(key, axis), (), 0, length) for axis, length in enumerate(result.shape)]
    widest = result.shape.index(max(result.shape))
    neighbour = spot[:widest] + [(spot[widest] + 1) % result.shape[widest]] + spot[widest + 1:]
    return result.at[tuple(spot)].set(low).at[tuple(neighbour)].set(largest)


def block_levels(key, dims, pieces, low, largest):
    factor_of = 1.0
    for axis_at, parts in pieces:
        steps = jax.random.uniform(jax.random.fold_in(jax.random.fold_in(key, 6), axis_at), (parts,), jnp.float32, low / len(pieces), largest / len(pieces))
        factor_of = factor_of * jnp.repeat(jnp.exp(steps), dims[axis_at] // parts).reshape((-1,) + (1,) * (len(dims) - 1 - axis_at))
    return factor_of


def bell_draw(own_key, extent, deviation, most, shards=(), kind=jnp.bfloat16):
    entries = deviation * jax.random.normal(own_key, extent, jnp.float32)
    if shards:
        entries = entries * block_levels(own_key, extent, shards, -0.22, 0.18)
    return jnp.clip(entries, -most, most).astype(kind)


def setup_inputs(seed: int = 0) -> dict:
    streams_of = jax.random.split(jax.random.key(seed), 8)
    return {
        "sensed_flows_levels": bell_draw(streams_of[0], (TOTAL_STEPS, MEASURE_COUNT), 1.0, 6.0, ((0, 8),), jnp.float32),
        "reading_mask": touch_ends((jax.random.randint(streams_of[1], (TOTAL_STEPS, MEASURE_COUNT), 0, 4) < 3).astype(jnp.int32), jax.random.fold_in(streams_of[1], 1), 0, 1),
        "inventory_propagator": draw_inventory_propagator(jax.random.fold_in(streams_of[7], 71), 0),
        "observation_matrix": bell_draw(streams_of[3], (MEASURE_COUNT, N), N ** -0.5, 0.1875, (), jnp.float32),
        "measurement_weight": jnp.clip(jax.random.uniform(streams_of[4], (MEASURE_COUNT,), jnp.float32, 0.05, 0.3), 0.05, 0.3),
        "diagonal_blend_factor": draw_diagonal_blend_factor(jax.random.fold_in(streams_of[7], 71), 0),
        "prior_inventory_mean": bell_draw(streams_of[6], (N,), 1.0, 6.0, (), jnp.float32),
    }


precise = lax.Precision.HIGHEST


def linear_map_apply(matrix, vector):
    return jnp.dot(matrix, vector, precision=precise, preferred_element_type=jnp.float32)


def reference(sensed_flows_levels, reading_mask, inventory_propagator, observation_matrix, measurement_weight, diagonal_blend_factor, prior_inventory_mean):
    blending_coefficients = reading_mask.astype(jnp.float32) * measurement_weight[None, :]

    def onward_pass_recursion(propagated_mean, inputs):
        measured, weight_row = inputs
        innovation = weight_row * (measured - linear_map_apply(observation_matrix, propagated_mean))
        current_mean = propagated_mean + jnp.dot(innovation, observation_matrix, precision=precise, preferred_element_type=jnp.float32)
        following = linear_map_apply(inventory_propagator, current_mean)
        return following, (current_mean, following)

    ignored_placeholder, (updated_inventory_means, prior_mean_single) = lax.scan(onward_pass_recursion, linear_map_apply(inventory_propagator, prior_inventory_mean), (sensed_flows_levels, blending_coefficients))

    def reverse_pass_recursion(later, inputs):
        state, propagated_mean, gain_vector = inputs
        current_mean = state + gain_vector * (later - propagated_mean)
        return current_mean, current_mean

    ignored_placeholder, reconciled_inventories = lax.scan(reverse_pass_recursion, prior_mean_single[-1], (updated_inventory_means, prior_mean_single, diagonal_blend_factor), reverse=True)
    return updated_inventory_means, reconciled_inventories
```

```python
import functools

import jax
import jax.numpy as jnp
from jax import lax
from jax.experimental import pallas as pl
from jax.experimental.pallas import tpu as pltpu
from jax.sharding import PartitionSpec as P

MESH = pl.DeviceIdType.MESH
CHUNK = 128
SHARES = (2, 0, 2)
PAIR = 2
SLOTS = 5


def turned(rows, by):
    return pltpu.roll(rows, by, 0)


def split_rows(rows):
    high = rows.astype(jnp.bfloat16).astype(jnp.float32)
    even = lax.broadcasted_iota(jnp.int32, rows.shape, 0) % 2 == 0
    return jnp.where(even, high, rows - high).astype(jnp.bfloat16)


def apply(rows, plain, high, low):
    outputs, depth = plain.shape
    if high is not None:
        left = split_rows(rows)
        upper = jnp.dot(left, high[...], preferred_element_type=jnp.float32)
        lower = jnp.dot(left, low[...], preferred_element_type=jnp.float32)
    parts = []
    for first in range(0, outputs, CHUNK):
        sums = None
        for at in range(0, depth, CHUNK):
            block = plain[first : first + CHUNK, at : at + CHUNK].reshape(CHUNK // 8, 8, CHUNK)
            term = block * rows[None, :, at : at + CHUNK]
            sums = term if sums is None else sums + term
        part = jnp.sum(sums.reshape(CHUNK, CHUNK).T.reshape(CHUNK // 8, 8, CHUNK), axis=0)
        for by in (4, 2, 1):
            part += turned(part, by)
        parts.append(part)
    if high is not None:
        total = upper + lower
        parts.append(total + turned(total, 1))
    return jnp.concatenate(parts, axis=1)


def matrix_part(size, eighths):
    return size * eighths // 8 // CHUNK * CHUNK


def halves(value):
    high = value.astype(jnp.bfloat16)
    return high, (value - high.astype(jnp.float32)).astype(jnp.bfloat16)


def kernel(
    z_ref, m_ref, f_hbm, h_hbm, mw_ref, g_ref, x0_ref,
    out_ref,
    z_all, m_all, g_all, f_in, h_in, ft_hi, ft_lo, ht_hi, ht_lo, h_hi, h_lo, ht_in, xs, ps,
    send_sem, recv_sem, load_sem,
):
    me = lax.axis_index("tm")
    count = lax.axis_size("tm")
    steps = z_ref.shape[0]
    width = f_hbm.shape[0]
    measures = h_hbm.shape[0]
    own = g_ref.shape[1]
    f_chunks, h_chunks = width // CHUNK, measures // CHUNK

    def load(c):
        if c < h_chunks:
            rows = pl.ds(c * CHUNK, CHUNK)
            return pltpu.make_async_copy(h_hbm.at[rows], h_in.at[rows], load_sem.at[c])
        rows = pl.ds((c - h_chunks) * CHUNK, CHUNK)
        return pltpu.make_async_copy(f_hbm.at[rows], f_in.at[rows], load_sem.at[c])

    for c in range(f_chunks + h_chunks):
        load(c).start()

    lane, row, last = lax.rem(me, PAIR), me // PAIR, count // PAIR - 1
    partner = me + 1 - PAIR * lane
    around = (
        (row >= 0, partner, (0, 1, 2)),
        (row < last, me + PAIR, (0, 1)),
        (row < last, partner + PAIR, (0, 1)),
        (row > 0, me - PAIR, (0, 1, 2)),
        (row > 0, partner - PAIR, (0, 1, 2)),
    )
    barrier = pltpu.get_barrier_semaphore()
    for there, peer, _ in around:

        @pl.when(there)
        def _():
            pl.semaphore_signal(barrier, inc=1, device_id={"tm": peer}, device_id_type=MESH)

    pl.semaphore_wait(barrier, 1 + PAIR * (lax.min(row, 1) + lax.min(last - row, 1)))

    pairs = ((z_ref, z_all), (m_ref, m_all), (g_ref, g_all))

    def send(i, slot, peer):
        return pltpu.make_async_remote_copy(
            src_ref=pairs[i][0], dst_ref=pairs[i][1].at[me],
            send_sem=send_sem.at[i, slot], recv_sem=recv_sem.at[i, me],
            device_id={"tm": peer}, device_id_type=MESH,
        )

    def relay(i, t, peer):
        return pltpu.make_async_remote_copy(
            src_ref=pairs[i][1].at[t], dst_ref=pairs[i][1].at[t],
            send_sem=send_sem.at[i, SLOTS + t], recv_sem=recv_sem.at[i, t],
            device_id={"tm": peer}, device_id_type=MESH,
        )

    def arrival(i, t):
        return pltpu.make_async_remote_copy(
            src_ref=pairs[i][0], dst_ref=pairs[i][1].at[t],
            send_sem=send_sem.at[i, 0], recv_sem=recv_sem.at[i, t],
            device_id={"tm": partner}, device_id_type=MESH,
        )

    for slot, (there, peer, items) in enumerate(around):

        @pl.when(there)
        def _():
            for i in items:
                send(i, slot, peer).start()

    def take_lower(onward):
        @pl.loop(1, row + 1)
        def _(d):
            for side in range(PAIR):
                t = PAIR * (row - d) + side
                for i in (0, 1):
                    arrival(i, t).wait_recv()
                    if onward:
                        relay(i, t, me + PAIR).start()

    def take_upper(d):
        for side in range(PAIR):
            t = PAIR * (row + d) + side
            for i in range(3):
                arrival(i, t).wait_recv()

            @pl.when(row > 0)
            def _():
                for i in range(3):
                    relay(i, t, me - PAIR).start()

    z_all[me] = z_ref[...]
    m_all[me] = m_ref[...]
    g_all[me] = g_ref[...]

    f_part, q_part, u_part = shares(width, measures)
    f_plain, q_plain, u_plain = width - f_part, measures - q_part, width - u_part
    for c in range(h_chunks):
        load(c).wait()
        rows = pl.ds(c * CHUNK, CHUNK)
        ht_in[:, rows] = h_in[rows, :u_plain].T
        if u_part:
            h_hi[rows, :], h_lo[rows, :] = halves(h_in[rows, u_plain:])
        if c * CHUNK >= q_plain:
            to = pl.ds(c * CHUNK - q_plain, CHUNK)
            ht_hi[:, to], ht_lo[:, to] = halves(h_in[rows, :].T)

    @pl.when(row < last)
    def _():
        take_lower(True)

    for c in range(f_chunks):
        load(h_chunks + c).wait()
        if c * CHUNK >= f_plain:
            to = pl.ds(c * CHUNK - f_plain, CHUNK)
            ft_hi[:, to], ft_lo[:, to] = halves(f_in[pl.ds(c * CHUNK, CHUNK), :].T)

    nothing = (None, None)
    propagate = (f_in.at[:f_plain], *((ft_hi, ft_lo) if f_part else nothing))
    observe = (h_in.at[:q_plain], *((ht_hi, ht_lo) if q_part else nothing))
    spread = (ht_in, *((h_hi, h_lo) if u_part else nothing))

    def block_of_steps(t, predicted):
        @pl.when((lax.rem(t, PAIR) == 1) & (row + (t + 1) // PAIR <= last))
        def _():
            take_upper((t + 1) // PAIR)

        weights = m_all[t].astype(jnp.float32) * mw_ref[...]
        readings = z_all[t]
        alike = functools.partial(jnp.broadcast_to, shape=(8, measures))
        for k in range(steps):
            seen = apply(predicted, *observe)
            change = alike(weights[k : k + 1]) * (alike(readings[k : k + 1]) - seen)
            state = predicted + apply(change, *spread)
            predicted = apply(state, *propagate)
            xs[t, k : k + 1, :] = state[:1]
            ps[t, k : k + 1, :] = predicted[:1]
        return predicted

    first = apply(jnp.broadcast_to(x0_ref[...], (8, width)), *propagate)

    @pl.when(row == last)
    def _():
        take_lower(False)

    for i in range(3):
        arrival(i, partner).wait_recv()

    lax.fori_loop(0, count, block_of_steps, first)

    columns = pl.ds(pl.multiple_of(lax.axis_index("rows") * own, own), own)

    def smooth(lap, later):
        t = count - 1 - lap
        means = xs[t, :, columns]
        priors = ps[t, :, columns]
        gains = g_all[t]
        rows = []
        for k in reversed(range(steps)):
            later = means[k : k + 1] + gains[k : k + 1] * (later - priors[k : k + 1])
            rows.insert(0, later)

        @pl.when(t == me)
        def _():
            out_ref[0] = means
            for k in range(steps):
                out_ref[1, k : k + 1, :] = rows[k]

        return later

    lax.fori_loop(0, count - me, smooth, ps[count - 1, steps - 1 : steps, columns])

    for slot, (there, peer, items) in enumerate(around):

        @pl.when(there)
        def _():
            for i in items:
                send(i, slot, peer).wait_send()

    @pl.when(row < last)
    def _():
        @pl.loop(0, PAIR * row)
        def _(t):
            for i in (0, 1):
                relay(i, t, me + PAIR).wait_send()

    @pl.when(row > 0)
    def _():
        @pl.loop(PAIR * (row + 1), count)
        def _(t):
            for i in range(3):
                relay(i, t, me - PAIR).wait_send()


def shares(width, measures):
    return tuple(map(matrix_part, (width, measures, width), SHARES))


def parted(both_ref, mean_ref, rec_ref):
    mean_ref[...] = both_ref[0]
    rec_ref[...] = both_ref[1]


def body(z, mask, f, h, mw, gain, x0):
    count = lax.axis_size("tm")
    steps, measures = z.shape
    width = f.shape[0]
    own = gain.shape[1]
    vmem = pl.BlockSpec(memory_space=pltpu.VMEM)
    hbm = pl.BlockSpec(memory_space=pl.ANY)
    out = jax.ShapeDtypeStruct((steps, own), jnp.float32)
    half = jnp.bfloat16
    f_part, q_part, u_part = shares(width, measures)
    both = pl.pallas_call(
        kernel,
        out_shape=jax.ShapeDtypeStruct((2, steps, own), jnp.float32),
        in_specs=[vmem, vmem, hbm, hbm, vmem, vmem, vmem],
        out_specs=vmem,
        scratch_shapes=[
            pltpu.VMEM((count, steps, measures), jnp.float32),
            pltpu.VMEM((count, steps, measures), jnp.int32),
            pltpu.VMEM((count, steps, own), jnp.float32),
            pltpu.VMEM((width, width), jnp.float32),
            pltpu.VMEM((measures, width), jnp.float32),
            pltpu.VMEM((width, max(f_part, CHUNK)), half),
            pltpu.VMEM((width, max(f_part, CHUNK)), half),
            pltpu.VMEM((width, max(q_part, CHUNK)), half),
            pltpu.VMEM((width, max(q_part, CHUNK)), half),
            pltpu.VMEM((measures, max(u_part, CHUNK)), half),
            pltpu.VMEM((measures, max(u_part, CHUNK)), half),
            pltpu.VMEM((width - u_part, measures), jnp.float32),
            pltpu.VMEM((count, steps, width), jnp.float32),
            pltpu.VMEM((count, steps, width), jnp.float32),
            pltpu.SemaphoreType.DMA((3, SLOTS + count)),
            pltpu.SemaphoreType.DMA((3, count)),
            pltpu.SemaphoreType.DMA(((width + measures) // CHUNK,)),
        ],
        compiler_params=pltpu.CompilerParams(
            collective_id=0, has_side_effects=True, vmem_limit_bytes=60 * 2**20
        ),
    )(z, mask, f, h, mw.reshape(1, -1), gain, x0.reshape(1, -1))
    return pl.pallas_call(
        parted, out_shape=(out, out), in_specs=[vmem], out_specs=(vmem, vmem)
    )(both)


def solution(mesh):
    placed = (P("tm", None), P("tm", None), P(), P(), P(), P("tm", "rows"), P())
    return jax.shard_map(
        body,
        mesh=mesh,
        in_specs=placed,
        out_specs=(P("tm", "rows"), P("tm", "rows")),
        check_vma=False,
    )
```

```python
import functools

import jax
import jax.numpy as jnp
from jax import lax
from jax.experimental import pallas as pl
from jax.experimental.pallas import tpu as pltpu
from jax.sharding import PartitionSpec as P

MESH = pl.DeviceIdType.MESH
CHUNK = 128
SHARES = (2, 0, 2)


def turned(rows, by):
    return pltpu.roll(rows, by, 0)


def split_rows(rows):
    high = rows.astype(jnp.bfloat16).astype(jnp.float32)
    even = lax.broadcasted_iota(jnp.int32, rows.shape, 0) % 2 == 0
    return jnp.where(even, high, rows - high).astype(jnp.bfloat16)


def apply(rows, plain, high, low):
    outputs, depth = plain.shape
    if high is not None:
        left = split_rows(rows)
        upper = jnp.dot(left, high[...], preferred_element_type=jnp.float32)
        lower = jnp.dot(left, low[...], preferred_element_type=jnp.float32)
    parts = []
    for first in range(0, outputs, CHUNK):
        sums = None
        for at in range(0, depth, CHUNK):
            block = plain[first : first + CHUNK, at : at + CHUNK].reshape(CHUNK // 8, 8, CHUNK)
            term = block * rows[None, :, at : at + CHUNK]
            sums = term if sums is None else sums + term
        part = jnp.sum(sums.reshape(CHUNK, CHUNK).T.reshape(CHUNK // 8, 8, CHUNK), axis=0)
        for by in (4, 2, 1):
            part += turned(part, by)
        parts.append(part)
    if high is not None:
        total = upper + lower
        parts.append(total + turned(total, 1))
    return jnp.concatenate(parts, axis=1)


def matrix_part(size, eighths):
    return size * eighths // 8 // CHUNK * CHUNK


def halves(value):
    high = value.astype(jnp.bfloat16)
    return high, (value - high.astype(jnp.float32)).astype(jnp.bfloat16)


def kernel(
    z_ref, m_ref, f_hbm, h_hbm, mw_hbm, g_ref, x0_hbm,
    out_ref,
    mw_ref, x0_ref, z_all, m_all, g_all, f_in, h_in, ft_hi, ft_lo, ht_hi, ht_lo, h_hi, h_lo, ht_in, xs, ps,
    send_sem, recv_sem, load_sem, own_sem,
):
    me = lax.axis_index("tm")
    count = lax.axis_size("tm")
    steps = z_ref.shape[0]
    width = f_hbm.shape[0]
    measures = h_hbm.shape[0]
    own = g_ref.shape[1]
    f_chunks, h_chunks = width // CHUNK, measures // CHUNK

    def load(c):
        if c < h_chunks:
            rows = pl.ds(c * CHUNK, CHUNK)
            return pltpu.make_async_copy(h_hbm.at[rows], h_in.at[rows], load_sem.at[c])
        rows = pl.ds((c - h_chunks) * CHUNK, CHUNK)
        return pltpu.make_async_copy(f_hbm.at[rows], f_in.at[rows], load_sem.at[c])

    barrier = pltpu.get_barrier_semaphore()

    @pl.loop(1, count)
    def _(d):
        peer = lax.rem(me + d, count)
        pl.semaphore_signal(barrier, inc=1, device_id={"tm": peer}, device_id_type=MESH)

    pairs = ((z_ref, z_all), (m_ref, m_all), (g_ref, g_all))
    loads = [(source, target.at[me]) for source, target in pairs] + [(mw_hbm, mw_ref), (x0_hbm, x0_ref)]
    own_loads = [pltpu.make_async_copy(*ends, own_sem.at[n]) for n, ends in enumerate(loads)]
    for c in range(f_chunks + h_chunks):
        load(c).start()
    for copy in own_loads:
        copy.start()
    pl.semaphore_wait(barrier, count - 1)

    def send(i, d):
        peer = lax.rem(me + d, count)
        return pltpu.make_async_remote_copy(
            src_ref=pairs[i][0], dst_ref=pairs[i][1].at[me],
            send_sem=send_sem.at[i, d], recv_sem=recv_sem.at[i, me],
            device_id={"tm": peer}, device_id_type=MESH,
        )

    def arrival(i, t):
        return pltpu.make_async_remote_copy(
            src_ref=pairs[i][0], dst_ref=pairs[i][1].at[t],
            send_sem=send_sem.at[i, 0], recv_sem=recv_sem.at[i, t],
            device_id={"tm": lax.rem(me + 1, count)}, device_id_type=MESH,
        )

    @pl.loop(1, count)
    def _(d):
        for i in range(3):
            send(i, d).start()

    for copy in own_loads:
        copy.wait()

    f_part, q_part, u_part = shares(width, measures)
    f_plain, q_plain, u_plain = width - f_part, measures - q_part, width - u_part
    for c in range(h_chunks):
        load(c).wait()
        rows = pl.ds(c * CHUNK, CHUNK)
        ht_in[:, rows] = h_in[rows, :u_plain].T
        if u_part:
            h_hi[rows, :], h_lo[rows, :] = halves(h_in[rows, u_plain:])
        if c * CHUNK >= q_plain:
            to = pl.ds(c * CHUNK - q_plain, CHUNK)
            ht_hi[:, to], ht_lo[:, to] = halves(h_in[rows, :].T)
    for c in range(f_chunks):
        load(h_chunks + c).wait()
        if c * CHUNK >= f_plain:
            to = pl.ds(c * CHUNK - f_plain, CHUNK)
            ft_hi[:, to], ft_lo[:, to] = halves(f_in[pl.ds(c * CHUNK, CHUNK), :].T)

    nothing = (None, None)
    propagate = (f_in.at[:f_plain], *((ft_hi, ft_lo) if f_part else nothing))
    observe = (h_in.at[:q_plain], *((ht_hi, ht_lo) if q_part else nothing))
    spread = (ht_in, *((h_hi, h_lo) if u_part else nothing))

    def block_of_steps(t, predicted):
        @pl.when(t != me)
        def _():
            arrival(0, t).wait_recv()
            arrival(1, t).wait_recv()

        weights = m_all[t].astype(jnp.float32) * mw_ref[...]
        readings = z_all[t]
        alike = functools.partial(jnp.broadcast_to, shape=(8, measures))
        for k in range(steps):
            seen = apply(predicted, *observe)
            change = alike(weights[k : k + 1]) * (alike(readings[k : k + 1]) - seen)
            state = predicted + apply(change, *spread)
            predicted = apply(state, *propagate)
            xs[t, k : k + 1, :] = state[:1]
            ps[t, k : k + 1, :] = predicted[:1]
        return predicted

    lax.fori_loop(0, count, block_of_steps, apply(jnp.broadcast_to(x0_ref[...], (8, width)), *propagate))

    columns = pl.ds(pl.multiple_of(lax.axis_index("rows") * own, own), own)

    @pl.loop(0, count)
    def _(t):
        @pl.when(t != me)
        def _():
            arrival(2, t).wait_recv()

    def smooth(lap, later):
        t = count - 1 - lap
        means = xs[t, :, columns]
        priors = ps[t, :, columns]
        gains = g_all[t]
        rows = []
        for k in reversed(range(steps)):
            later = means[k : k + 1] + gains[k : k + 1] * (later - priors[k : k + 1])
            rows.insert(0, later)

        @pl.when(t == me)
        def _():
            out_ref[0] = means
            for k in range(steps):
                out_ref[1, k : k + 1, :] = rows[k]

        return later

    lax.fori_loop(0, count - me, smooth, ps[count - 1, steps - 1 : steps, columns])

    @pl.loop(1, count)
    def _(d):
        for i in range(3):
            send(i, d).wait_send()


def shares(width, measures):
    return tuple(map(matrix_part, (width, measures, width), SHARES))


def parted(both_ref, mean_ref, rec_ref):
    mean_ref[...] = both_ref[0]
    rec_ref[...] = both_ref[1]


def body(z, mask, f, h, mw, gain, x0):
    count = lax.axis_size("tm")
    steps, measures = z.shape
    width = f.shape[0]
    own = gain.shape[1]
    vmem = pl.BlockSpec(memory_space=pltpu.VMEM)
    hbm = pl.BlockSpec(memory_space=pltpu.HBM)
    out = jax.ShapeDtypeStruct((steps, own), jnp.float32)
    half = jnp.bfloat16
    f_part, q_part, u_part = shares(width, measures)
    both = pl.pallas_call(
        kernel,
        out_shape=jax.ShapeDtypeStruct((2, steps, own), jnp.float32),
        in_specs=[hbm] * 7,
        out_specs=vmem,
        scratch_shapes=[
            pltpu.VMEM((1, measures), jnp.float32),
            pltpu.VMEM((1, width), jnp.float32),
            pltpu.VMEM((count, steps, measures), jnp.float32),
            pltpu.VMEM((count, steps, measures), jnp.int32),
            pltpu.VMEM((count, steps, own), jnp.float32),
            pltpu.VMEM((width, width), jnp.float32),
            pltpu.VMEM((measures, width), jnp.float32),
            pltpu.VMEM((width, max(f_part, CHUNK)), half),
            pltpu.VMEM((width, max(f_part, CHUNK)), half),
            pltpu.VMEM((width, max(q_part, CHUNK)), half),
            pltpu.VMEM((width, max(q_part, CHUNK)), half),
            pltpu.VMEM((measures, max(u_part, CHUNK)), half),
            pltpu.VMEM((measures, max(u_part, CHUNK)), half),
            pltpu.VMEM((width - u_part, measures), jnp.float32),
            pltpu.VMEM((count, steps, width), jnp.float32),
            pltpu.VMEM((count, steps, width), jnp.float32),
            pltpu.SemaphoreType.DMA((3, count)),
            pltpu.SemaphoreType.DMA((3, count)),
            pltpu.SemaphoreType.DMA(((width + measures) // CHUNK,)),
            pltpu.SemaphoreType.DMA((5,)),
        ],
        compiler_params=pltpu.CompilerParams(
            collective_id=0, has_side_effects=True, vmem_limit_bytes=60 * 2**20
        ),
    )(z, mask, f, h, mw.reshape(1, -1), gain, x0.reshape(1, -1))
    return pl.pallas_call(
        parted, out_shape=(out, out), in_specs=[vmem], out_specs=(vmem, vmem)
    )(both)


def solution(mesh):
    placed = (P("tm", None), P("tm", None), P(), P(), P(), P("tm", "rows"), P())
    return jax.shard_map(
        body,
        mesh=mesh,
        in_specs=placed,
        out_specs=(P("tm", "rows"), P("tm", "rows")),
        check_vma=False,
    )
```

```python
import functools

import jax
import jax.numpy as jnp
from jax import lax
from jax.experimental import pallas as pl
from jax.experimental.pallas import tpu as pltpu
from jax.sharding import PartitionSpec as P

MESH = pl.DeviceIdType.MESH
CHUNK = 128
BAND = 256
PUSH_AT = 3
SHARES = (4, 2)


def turned(rows, by):
    return pltpu.roll(rows, by, 0)


def split_rows(rows):
    high = rows.astype(jnp.bfloat16).astype(jnp.float32)
    even = lax.broadcasted_iota(jnp.int32, rows.shape, 0) % 2 == 0
    return jnp.where(even, high, rows - high).astype(jnp.bfloat16)


def apply(rows, plain, firsts, high, low):
    depth = plain.shape[1]
    if high is not None:
        left = split_rows(rows)
        upper = jnp.dot(left, high[...], preferred_element_type=jnp.float32)
        lower = jnp.dot(left, low[...], preferred_element_type=jnp.float32)
    parts = []
    for first in firsts:
        sums = None
        for at in range(0, depth, CHUNK):
            block = plain[first : first + CHUNK, at : at + CHUNK].reshape(CHUNK // 8, 8, CHUNK)
            term = block * rows[None, :, at : at + CHUNK]
            sums = term if sums is None else sums + term
        part = jnp.sum(sums.reshape(CHUNK, CHUNK).T.reshape(CHUNK // 8, 8, CHUNK), axis=0)
        for by in (4, 2, 1):
            part += turned(part, by)
        parts.append(part)
    if high is None:
        return parts, []
    total = upper + lower
    return parts, [total + turned(total, 1)]


def matrix_part(size, eighths):
    return size * eighths // 8 // CHUNK * CHUNK


def halves(value):
    high = value.astype(jnp.bfloat16)
    return high, (value - high.astype(jnp.float32)).astype(jnp.bfloat16)


def kernel(
    z_ref, m_ref, f_hbm, h_hbm, mw_hbm, g_ref, x0_hbm,
    out_ref,
    mw_ref, x0_ref, z_all, m_all, g_all, gf, h_in, band_hi, band_lo, ft_hi, ft_lo, h_hi, h_lo, ht_in, xs, ps,
    send_sem, recv_sem, load_sem, own_sem,
):
    me = lax.axis_index("tm")
    count = lax.axis_size("tm")
    steps = z_ref.shape[0]
    width = f_hbm.shape[0]
    measures = h_hbm.shape[0]
    own = g_ref.shape[1]
    f_chunks, h_chunks = width // CHUNK, measures // CHUNK

    def load(c):
        if c < h_chunks:
            rows = pl.ds(c * CHUNK, CHUNK)
            return pltpu.make_async_copy(h_hbm.at[rows], h_in.at[rows], load_sem.at[c])
        rows = pl.ds((c - h_chunks) * CHUNK, CHUNK)
        target = gf.at[pl.ds(measures + (c - h_chunks) * CHUNK, CHUNK)]
        return pltpu.make_async_copy(f_hbm.at[rows], target, load_sem.at[c])

    barrier = pltpu.get_barrier_semaphore()

    @pl.loop(1, count)
    def _(d):
        peer = lax.rem(me + d, count)
        pl.semaphore_signal(barrier, inc=1, device_id={"tm": peer}, device_id_type=MESH)

    pairs = ((z_ref, z_all), (m_ref, m_all), (g_ref, g_all))
    loads = [(source, target.at[me]) for source, target in pairs] + [(mw_hbm, mw_ref), (x0_hbm, x0_ref)]
    own_loads = [pltpu.make_async_copy(*ends, own_sem.at[n]) for n, ends in enumerate(loads)]
    for c in range(f_chunks + h_chunks):
        load(c).start()
    for copy in own_loads:
        copy.start()
    for copy in own_loads:
        copy.wait()

    def send(i, peer):
        return pltpu.make_async_remote_copy(
            src_ref=pairs[i][0], dst_ref=pairs[i][1].at[me],
            send_sem=send_sem.at[i, peer], recv_sem=recv_sem.at[i, me],
            device_id={"tm": peer}, device_id_type=MESH,
        )

    def arrival(i, t):
        return pltpu.make_async_remote_copy(
            src_ref=pairs[i][0], dst_ref=pairs[i][1].at[t],
            send_sem=send_sem.at[i, 0], recv_sem=recv_sem.at[i, t],
            device_id={"tm": lax.rem(me + 1, count)}, device_id_type=MESH,
        )

    def push():
        pl.semaphore_wait(barrier, count - 1)

        @pl.loop(1, count)
        def _(d):
            peer = lax.rem(me + count - d, count)
            for i in (0, 1):
                send(i, peer).start()

        @pl.loop(0, me)
        def _(peer):
            send(2, peer).start()

    f_part, u_part = shares(width)
    u_plain = width - u_part
    bands = width // BAND
    for c in range(h_chunks):
        load(c).wait()
        rows = pl.ds(c * CHUNK, CHUNK)
        ht_in[:, rows] = h_in[rows, :u_plain].T
        if u_part:
            h_hi[rows, :], h_lo[rows, :] = halves(h_in[rows, u_plain:])
        for b in range(bands):
            band_hi[b, rows, :], band_lo[b, rows, :] = halves(h_in[rows, b * BAND : (b + 1) * BAND])
    for b in range(bands):
        if b == PUSH_AT:
            push()
        for c in range(b * BAND // CHUNK, (b + 1) * BAND // CHUNK):
            load(h_chunks + c).wait()
        high, low = halves(gf[measures + b * BAND : measures + (b + 1) * BAND, :])
        product = functools.partial(jnp.dot, preferred_element_type=jnp.float32)
        term = product(band_hi[b], high) + product(band_lo[b], high) + product(band_hi[b], low)
        gf[:measures, :] = term if b == 0 else gf[:measures, :] + term
        for first in range(b * BAND, min((b + 1) * BAND, f_part), CHUNK):
            to = pl.ds(first, CHUNK)
            ft_hi[:, to], ft_lo[:, to] = halves(gf[measures + first : measures + first + CHUNK, :].T)

    def advance(state):
        firsts = [*range(0, measures, CHUNK), *range(measures + f_part, measures + width, CHUNK)]
        parts, shared = apply(state, gf, firsts, *((ft_hi, ft_lo) if f_part else (None, None)))
        seen = jnp.concatenate(parts[: measures // CHUNK], axis=1)
        return jnp.concatenate([*shared, *parts[measures // CHUNK :]], axis=1), seen

    def spread(change):
        parts, shared = apply(
            change, ht_in, range(0, u_plain, CHUNK), *((h_hi, h_lo) if u_part else (None, None))
        )
        return jnp.concatenate([*parts, *shared], axis=1)

    def block_of_steps(t, carried):
        predicted, seen = carried

        @pl.when(t != me)
        def _():
            arrival(0, t).wait_recv()
            arrival(1, t).wait_recv()

        weights = m_all[t].astype(jnp.float32) * mw_ref[...]
        readings = z_all[t]
        alike = functools.partial(jnp.broadcast_to, shape=(8, measures))
        for k in range(steps):
            change = alike(weights[k : k + 1]) * (alike(readings[k : k + 1]) - seen)
            state = predicted + spread(change)
            predicted, seen = advance(state)
            xs[t, k : k + 1, :] = state[:1]
            ps[t, k : k + 1, :] = predicted[:1]
        return predicted, seen

    lax.fori_loop(0, count, block_of_steps, advance(jnp.broadcast_to(x0_ref[...], (8, width))))

    columns = pl.ds(pl.multiple_of(lax.axis_index("rows") * own, own), own)

    @pl.loop(me + 1, count)
    def _(t):
        arrival(2, t).wait_recv()

    def smooth(lap, later):
        t = count - 1 - lap
        means = xs[t, :, columns]
        priors = ps[t, :, columns]
        gains = g_all[t]
        rows = []
        for k in reversed(range(steps)):
            later = means[k : k + 1] + gains[k : k + 1] * (later - priors[k : k + 1])
            rows.insert(0, later)

        @pl.when(t == me)
        def _():
            out_ref[0] = means
            for k in range(steps):
                out_ref[1, k : k + 1, :] = rows[k]

        return later

    lax.fori_loop(0, count - me, smooth, ps[count - 1, steps - 1 : steps, columns])

    @pl.loop(1, count)
    def _(d):
        for i in (0, 1):
            send(i, lax.rem(me + count - d, count)).wait_send()

    @pl.loop(0, me)
    def _(peer):
        send(2, peer).wait_send()


def shares(width):
    return tuple(matrix_part(width, eighths) for eighths in SHARES)


def parted(both_ref, mean_ref, rec_ref):
    mean_ref[...] = both_ref[0]
    rec_ref[...] = both_ref[1]


def body(z, mask, f, h, mw, gain, x0):
    count = lax.axis_size("tm")
    steps, measures = z.shape
    width = f.shape[0]
    own = gain.shape[1]
    vmem = pl.BlockSpec(memory_space=pltpu.VMEM)
    hbm = pl.BlockSpec(memory_space=pltpu.HBM)
    out = jax.ShapeDtypeStruct((steps, own), jnp.float32)
    half = jnp.bfloat16
    f_part, u_part = shares(width)
    both = pl.pallas_call(
        kernel,
        out_shape=jax.ShapeDtypeStruct((2, steps, own), jnp.float32),
        in_specs=[hbm] * 7,
        out_specs=vmem,
        scratch_shapes=[
            pltpu.VMEM((1, measures), jnp.float32),
            pltpu.VMEM((1, width), jnp.float32),
            pltpu.VMEM((count, steps, measures), jnp.float32),
            pltpu.VMEM((count, steps, measures), jnp.int32),
            pltpu.VMEM((count, steps, own), jnp.float32),
            pltpu.VMEM((measures + width, width), jnp.float32),
            pltpu.VMEM((measures, width), jnp.float32),
            pltpu.VMEM((width // BAND, measures, BAND), half),
            pltpu.VMEM((width // BAND, measures, BAND), half),
            pltpu.VMEM((width, max(f_part, CHUNK)), half),
            pltpu.VMEM((width, max(f_part, CHUNK)), half),
            pltpu.VMEM((measures, max(u_part, CHUNK)), half),
            pltpu.VMEM((measures, max(u_part, CHUNK)), half),
            pltpu.VMEM((width - u_part, measures), jnp.float32),
            pltpu.VMEM((count, steps, width), jnp.float32),
            pltpu.VMEM((count, steps, width), jnp.float32),
            pltpu.SemaphoreType.DMA((3, count)),
            pltpu.SemaphoreType.DMA((3, count)),
            pltpu.SemaphoreType.DMA(((width + measures) // CHUNK,)),
            pltpu.SemaphoreType.DMA((5,)),
        ],
        compiler_params=pltpu.CompilerParams(
            collective_id=0, has_side_effects=True, vmem_limit_bytes=60 * 2**20
        ),
    )(z, mask, f, h, mw.reshape(1, -1), gain, x0.reshape(1, -1))
    return pl.pallas_call(
        parted, out_shape=(out, out), in_specs=[vmem], out_specs=(vmem, vmem)
    )(both)


def solution(mesh):
    placed = (P("tm", None), P("tm", None), P(), P(), P(), P("tm", "rows"), P())
    return jax.shard_map(
        body,
        mesh=mesh,
        in_specs=placed,
        out_specs=(P("tm", "rows"), P("tm", "rows")),
        check_vma=False,
    )
```

```python
import functools

import jax
import jax.numpy as jnp
from jax import lax
from jax.experimental import pallas as pl
from jax.experimental.pallas import tpu as pltpu
from jax.sharding import PartitionSpec as P

MESH = pl.DeviceIdType.MESH
CHUNK = 128
BAND = 256
PUSH_AT = 2
SHARES = (4, 2)


def turned(rows, by):
    return pltpu.roll(rows, by, 0)


def split_rows(rows):
    high = rows.astype(jnp.bfloat16).astype(jnp.float32)
    even = lax.broadcasted_iota(jnp.int32, rows.shape, 0) % 2 == 0
    return jnp.where(even, high, rows - high).astype(jnp.bfloat16)


def apply(rows, plain, firsts, high, low):
    depth = plain.shape[1]
    if high is not None:
        left = split_rows(rows)
        upper = jnp.dot(left, high[...], preferred_element_type=jnp.float32)
        lower = jnp.dot(left, low[...], preferred_element_type=jnp.float32)
    parts = []
    for first in firsts:
        sums = None
        for at in range(0, depth, CHUNK):
            block = plain[first : first + CHUNK, at : at + CHUNK].reshape(CHUNK // 8, 8, CHUNK)
            term = block * rows[None, :, at : at + CHUNK]
            sums = term if sums is None else sums + term
        part = jnp.sum(sums.reshape(CHUNK, CHUNK).T.reshape(CHUNK // 8, 8, CHUNK), axis=0)
        for by in (4, 2, 1):
            part += turned(part, by)
        parts.append(part)
    if high is None:
        return parts, []
    total = upper + lower
    return parts, [total + turned(total, 1)]


def matrix_part(size, eighths):
    return size * eighths // 8 // CHUNK * CHUNK


def halves(value):
    high = value.astype(jnp.bfloat16)
    return high, (value - high.astype(jnp.float32)).astype(jnp.bfloat16)


def kernel(
    z_ref, m_ref, f_hbm, h_hbm, mw_hbm, g_ref, x0_hbm,
    out_ref,
    mw_ref, x0_ref, z_all, m_all, g_all, gf, h_in, ft_hi, ft_lo, h_hi, h_lo, ht_in, xs, ps,
    send_sem, recv_sem, load_sem, own_sem,
):
    me = lax.axis_index("tm")
    count = lax.axis_size("tm")
    steps = z_ref.shape[0]
    width = f_hbm.shape[0]
    measures = h_hbm.shape[0]
    own = g_ref.shape[1]
    f_chunks, h_chunks = width // CHUNK, measures // CHUNK

    def load(c):
        if c < h_chunks:
            rows = pl.ds(c * CHUNK, CHUNK)
            return pltpu.make_async_copy(h_hbm.at[rows], h_in.at[rows], load_sem.at[c])
        rows = pl.ds((c - h_chunks) * CHUNK, CHUNK)
        target = gf.at[pl.ds(measures + (c - h_chunks) * CHUNK, CHUNK)]
        return pltpu.make_async_copy(f_hbm.at[rows], target, load_sem.at[c])

    barrier = pltpu.get_barrier_semaphore()

    @pl.loop(1, count)
    def _(d):
        peer = lax.rem(me + d, count)
        pl.semaphore_signal(barrier, inc=1, device_id={"tm": peer}, device_id_type=MESH)

    pairs = ((z_ref, z_all), (m_ref, m_all), (g_ref, g_all))
    loads = [(source, target.at[me]) for source, target in pairs] + [(mw_hbm, mw_ref), (x0_hbm, x0_ref)]
    own_loads = [pltpu.make_async_copy(*ends, own_sem.at[n]) for n, ends in enumerate(loads)]
    for c in range(f_chunks + h_chunks):
        load(c).start()
    for copy in own_loads:
        copy.start()
    for copy in own_loads:
        copy.wait()

    def send(i, peer):
        return pltpu.make_async_remote_copy(
            src_ref=pairs[i][0], dst_ref=pairs[i][1].at[me],
            send_sem=send_sem.at[i, peer], recv_sem=recv_sem.at[i, me],
            device_id={"tm": peer}, device_id_type=MESH,
        )

    def arrival(i, t):
        return pltpu.make_async_remote_copy(
            src_ref=pairs[i][0], dst_ref=pairs[i][1].at[t],
            send_sem=send_sem.at[i, 0], recv_sem=recv_sem.at[i, t],
            device_id={"tm": lax.rem(me + 1, count)}, device_id_type=MESH,
        )

    def push():
        pl.semaphore_wait(barrier, count - 1)

        @pl.loop(1, count)
        def _(d):
            peer = lax.rem(me + count - d, count)
            for i in (0, 1):
                send(i, peer).start()

        @pl.loop(0, me)
        def _(peer):
            send(2, peer).start()

    f_part, u_part = shares(width)
    u_plain = width - u_part
    bands = width // BAND
    for c in range(h_chunks):
        load(c).wait()
    for b in range(bands):
        if b == PUSH_AT:
            push()
        if b <= PUSH_AT:
            for c in range(b * BAND // CHUNK, ((b + 1) if b < PUSH_AT else bands) * BAND // CHUNK):
                load(h_chunks + c).wait()
        high, low = halves(gf[measures + b * BAND : measures + (b + 1) * BAND, :])
        h_high, h_low = halves(h_in[:, b * BAND : (b + 1) * BAND])
        product = functools.partial(jnp.dot, preferred_element_type=jnp.float32)
        term = product(h_high, high) + product(h_low, high) + product(h_high, low)
        gf[:measures, :] = term if b == 0 else gf[:measures, :] + term
        if b == 0:
            ht_in[...] = h_in[:, :u_plain].T
            if u_part:
                h_hi[...], h_lo[...] = halves(h_in[:, u_plain:])
        for first in range(b * BAND, min((b + 1) * BAND, f_part), CHUNK):
            to = pl.ds(first, CHUNK)
            ft_hi[:, to], ft_lo[:, to] = halves(gf[measures + first : measures + first + CHUNK, :].T)

    def start(state):
        parts, _ = apply(state, gf, range(measures, measures + width, CHUNK), None, None)
        predicted = jnp.concatenate(parts, axis=1)
        parts, _ = apply(predicted, h_in, range(0, measures, CHUNK), None, None)
        return predicted, jnp.concatenate(parts, axis=1)

    def advance(state):
        firsts = [*range(0, measures, CHUNK), *range(measures + f_part, measures + width, CHUNK)]
        parts, shared = apply(state, gf, firsts, *((ft_hi, ft_lo) if f_part else (None, None)))
        seen = jnp.concatenate(parts[: measures // CHUNK], axis=1)
        return jnp.concatenate([*shared, *parts[measures // CHUNK :]], axis=1), seen

    def spread(change):
        parts, shared = apply(
            change, ht_in, range(0, u_plain, CHUNK), *((h_hi, h_lo) if u_part else (None, None))
        )
        return jnp.concatenate([*parts, *shared], axis=1)

    def block_of_steps(t, carried):
        predicted, seen = carried

        @pl.when(t != me)
        def _():
            arrival(0, t).wait_recv()
            arrival(1, t).wait_recv()

        weights = m_all[t].astype(jnp.float32) * mw_ref[...]
        readings = z_all[t]
        alike = functools.partial(jnp.broadcast_to, shape=(8, measures))
        for k in range(steps):
            change = alike(weights[k : k + 1]) * (alike(readings[k : k + 1]) - seen)
            state = predicted + spread(change)
            predicted, seen = advance(state)
            xs[t, k : k + 1, :] = state[:1]
            ps[t, k : k + 1, :] = predicted[:1]
        return predicted, seen

    lax.fori_loop(0, count, block_of_steps, start(jnp.broadcast_to(x0_ref[...], (8, width))))

    columns = pl.ds(pl.multiple_of(lax.axis_index("rows") * own, own), own)

    @pl.loop(me + 1, count)
    def _(t):
        arrival(2, t).wait_recv()

    def smooth(lap, later):
        t = count - 1 - lap
        means = xs[t, :, columns]
        priors = ps[t, :, columns]
        gains = g_all[t]
        rows = []
        for k in reversed(range(steps)):
            later = means[k : k + 1] + gains[k : k + 1] * (later - priors[k : k + 1])
            rows.insert(0, later)

        @pl.when(t == me)
        def _():
            out_ref[0] = means
            for k in range(steps):
                out_ref[1, k : k + 1, :] = rows[k]

        return later

    lax.fori_loop(0, count - me, smooth, ps[count - 1, steps - 1 : steps, columns])

    @pl.loop(1, count)
    def _(d):
        for i in (0, 1):
            send(i, lax.rem(me + count - d, count)).wait_send()

    @pl.loop(0, me)
    def _(peer):
        send(2, peer).wait_send()


def shares(width):
    return tuple(matrix_part(width, eighths) for eighths in SHARES)


def parted(both_ref, mean_ref, rec_ref):
    mean_ref[...] = both_ref[0]
    rec_ref[...] = both_ref[1]


def body(z, mask, f, h, mw, gain, x0):
    count = lax.axis_size("tm")
    steps, measures = z.shape
    width = f.shape[0]
    own = gain.shape[1]
    vmem = pl.BlockSpec(memory_space=pltpu.VMEM)
    hbm = pl.BlockSpec(memory_space=pltpu.HBM)
    out = jax.ShapeDtypeStruct((steps, own), jnp.float32)
    half = jnp.bfloat16
    f_part, u_part = shares(width)
    both = pl.pallas_call(
        kernel,
        out_shape=jax.ShapeDtypeStruct((2, steps, own), jnp.float32),
        in_specs=[hbm] * 7,
        out_specs=vmem,
        scratch_shapes=[
            pltpu.VMEM((1, measures), jnp.float32),
            pltpu.VMEM((1, width), jnp.float32),
            pltpu.VMEM((count, steps, measures), jnp.float32),
            pltpu.VMEM((count, steps, measures), jnp.int32),
            pltpu.VMEM((count, steps, own), jnp.float32),
            pltpu.VMEM((measures + width, width), jnp.float32),
            pltpu.VMEM((measures, width), jnp.float32),
            pltpu.VMEM((width, max(f_part, CHUNK)), half),
            pltpu.VMEM((width, max(f_part, CHUNK)), half),
            pltpu.VMEM((measures, max(u_part, CHUNK)), half),
            pltpu.VMEM((measures, max(u_part, CHUNK)), half),
            pltpu.VMEM((width - u_part, measures), jnp.float32),
            pltpu.VMEM((count, steps, width), jnp.float32),
            pltpu.VMEM((count, steps, width), jnp.float32),
            pltpu.SemaphoreType.DMA((3, count)),
            pltpu.SemaphoreType.DMA((3, count)),
            pltpu.SemaphoreType.DMA(((width + measures) // CHUNK,)),
            pltpu.SemaphoreType.DMA((5,)),
        ],
        compiler_params=pltpu.CompilerParams(
            collective_id=0, has_side_effects=True, vmem_limit_bytes=60 * 2**20
        ),
    )(z, mask, f, h, mw.reshape(1, -1), gain, x0.reshape(1, -1))
    return pl.pallas_call(
        parted, out_shape=(out, out), in_specs=[vmem], out_specs=(vmem, vmem)
    )(both)


def solution(mesh):
    placed = (P("tm", None), P("tm", None), P(), P(), P(), P("tm", "rows"), P())
    return jax.shard_map(
        body,
        mesh=mesh,
        in_specs=placed,
        out_specs=(P("tm", "rows"), P("tm", "rows")),
        check_vma=False,
    )
```

```python
import functools

import jax
import jax.numpy as jnp
from jax import lax
from jax.experimental import pallas as pl
from jax.experimental.pallas import tpu as pltpu
from jax.sharding import PartitionSpec as P

MESH = pl.DeviceIdType.MESH
CHUNK = 128
BAND = 256
PUSH_AT = 2
SHARES = (4, 1)


def turned(rows, by):
    return pltpu.roll(rows, by, 0)


def split_rows(rows):
    high = rows.astype(jnp.bfloat16).astype(jnp.float32)
    even = lax.broadcasted_iota(jnp.int32, rows.shape, 0) % 2 == 0
    return jnp.where(even, high, rows - high).astype(jnp.bfloat16)


def apply(rows, plain, firsts, high, low):
    depth = plain.shape[1]
    if high is not None:
        left = split_rows(rows)
        upper = jnp.dot(left, high[...], preferred_element_type=jnp.float32)
        lower = jnp.dot(left, low[...], preferred_element_type=jnp.float32)
    parts = []
    for first in firsts:
        sums = None
        for at in range(0, depth, CHUNK):
            block = plain[first : first + CHUNK, at : at + CHUNK].reshape(CHUNK // 8, 8, CHUNK)
            term = block * rows[None, :, at : at + CHUNK]
            sums = term if sums is None else sums + term
        part = jnp.sum(sums.reshape(CHUNK, CHUNK).T.reshape(CHUNK // 8, 8, CHUNK), axis=0)
        for by in (4, 2, 1):
            part += turned(part, by)
        parts.append(part)
    if high is None:
        return parts, []
    total = upper + lower
    return parts, [total + turned(total, 1)]


def matrix_part(size, eighths):
    return size * eighths // 8 // CHUNK * CHUNK


def halves(value):
    high = value.astype(jnp.bfloat16)
    return high, (value - high.astype(jnp.float32)).astype(jnp.bfloat16)


def kernel(
    z_ref, m_ref, f_hbm, h_hbm, mw_hbm, g_ref, x0_hbm,
    out_ref,
    mw_ref, x0_ref, z_all, m_all, g_all, gf, h_in, ft_hi, ft_lo, h_hi, h_lo, ht_in, xs, ps,
    send_sem, recv_sem, load_sem, own_sem,
):
    me = lax.axis_index("tm")
    count = lax.axis_size("tm")
    steps = z_ref.shape[0]
    width = f_hbm.shape[0]
    measures = h_hbm.shape[0]
    own = g_ref.shape[1]
    f_chunks, h_chunks = width // CHUNK, measures // CHUNK

    def load(c):
        if c < h_chunks:
            rows = pl.ds(c * CHUNK, CHUNK)
            return pltpu.make_async_copy(h_hbm.at[rows], h_in.at[rows], load_sem.at[c])
        rows = pl.ds((c - h_chunks) * CHUNK, CHUNK)
        target = gf.at[pl.ds(measures + (c - h_chunks) * CHUNK, CHUNK)]
        return pltpu.make_async_copy(f_hbm.at[rows], target, load_sem.at[c])

    barrier = pltpu.get_barrier_semaphore()

    @pl.loop(1, count)
    def _(d):
        peer = lax.rem(me + d, count)
        pl.semaphore_signal(barrier, inc=1, device_id={"tm": peer}, device_id_type=MESH)

    pairs = ((z_ref, z_all), (m_ref, m_all), (g_ref, g_all))
    loads = [(source, target.at[me]) for source, target in pairs] + [(mw_hbm, mw_ref), (x0_hbm, x0_ref)]
    own_loads = [pltpu.make_async_copy(*ends, own_sem.at[n]) for n, ends in enumerate(loads)]
    early = h_chunks + BAND // CHUNK
    for c in range(early):
        load(c).start()
    for copy in own_loads:
        copy.start()
    for copy in own_loads:
        copy.wait()

    def send(i, peer):
        return pltpu.make_async_remote_copy(
            src_ref=pairs[i][0], dst_ref=pairs[i][1].at[me],
            send_sem=send_sem.at[i, peer], recv_sem=recv_sem.at[i, me],
            device_id={"tm": peer}, device_id_type=MESH,
        )

    def arrival(i, t):
        return pltpu.make_async_remote_copy(
            src_ref=pairs[i][0], dst_ref=pairs[i][1].at[t],
            send_sem=send_sem.at[i, 0], recv_sem=recv_sem.at[i, t],
            device_id={"tm": lax.rem(me + 1, count)}, device_id_type=MESH,
        )

    def push():
        pl.semaphore_wait(barrier, count - 1)

        @pl.loop(1, count)
        def _(d):
            peer = lax.rem(me + d, count)
            for i in (0, 1):
                send(i, peer).start()

        @pl.loop(0, me)
        def _(peer):
            send(2, peer).start()

    f_part, u_part = shares(width)
    u_plain = width - u_part
    bands = width // BAND
    for c in range(h_chunks):
        load(c).wait()
    for b in range(bands):
        if b == PUSH_AT:
            push()
        if b <= PUSH_AT:
            for c in range(b * BAND // CHUNK, ((b + 1) if b < PUSH_AT else bands) * BAND // CHUNK):
                load(h_chunks + c).wait()
        if b == 0:
            for c in range(early, f_chunks + h_chunks):
                load(c).start()
        high, low = halves(gf[measures + b * BAND : measures + (b + 1) * BAND, :])
        h_high, h_low = halves(h_in[:, b * BAND : (b + 1) * BAND])
        product = functools.partial(jnp.dot, preferred_element_type=jnp.float32)
        term = product(
            jnp.concatenate([h_high, h_low, h_high], axis=1), jnp.concatenate([high, high, low], axis=0)
        )
        gf[:measures, :] = term if b == 0 else gf[:measures, :] + term
        if b == 0:
            ht_in[...] = h_in[:, :u_plain].T
            if u_part:
                h_hi[...], h_lo[...] = halves(h_in[:, u_plain:])
        for first in range(b * BAND, min((b + 1) * BAND, f_part), CHUNK):
            to = pl.ds(first, CHUNK)
            ft_hi[:, to], ft_lo[:, to] = halves(gf[measures + first : measures + first + CHUNK, :].T)

    def start(state):
        parts, _ = apply(state, gf, range(measures, measures + width, CHUNK), None, None)
        predicted = jnp.concatenate(parts, axis=1)
        parts, _ = apply(predicted, h_in, range(0, measures, CHUNK), None, None)
        return predicted, jnp.concatenate(parts, axis=1)

    def advance(state):
        firsts = [*range(0, measures, CHUNK), *range(measures + f_part, measures + width, CHUNK)]
        parts, shared = apply(state, gf, firsts, *((ft_hi, ft_lo) if f_part else (None, None)))
        seen = jnp.concatenate(parts[: measures // CHUNK], axis=1)
        return jnp.concatenate([*shared, *parts[measures // CHUNK :]], axis=1), seen

    def spread(change):
        parts, shared = apply(
            change, ht_in, range(0, u_plain, CHUNK), *((h_hi, h_lo) if u_part else (None, None))
        )
        return jnp.concatenate([*parts, *shared], axis=1)

    def block_of_steps(t, carried):
        predicted, seen = carried

        @pl.when(t != me)
        def _():
            arrival(0, t).wait_recv()
            arrival(1, t).wait_recv()

        weights = m_all[t].astype(jnp.float32) * mw_ref[...]
        readings = z_all[t]
        alike = functools.partial(jnp.broadcast_to, shape=(8, measures))
        for k in range(steps):
            change = alike(weights[k : k + 1]) * (alike(readings[k : k + 1]) - seen)
            state = predicted + spread(change)
            predicted, seen = advance(state)
            xs[t, k : k + 1, :] = state[:1]
            ps[t, k : k + 1, :] = predicted[:1]
        return predicted, seen

    lax.fori_loop(0, count, block_of_steps, start(jnp.broadcast_to(x0_ref[...], (8, width))))

    columns = pl.ds(pl.multiple_of(lax.axis_index("rows") * own, own), own)

    @pl.loop(me + 1, count)
    def _(t):
        arrival(2, t).wait_recv()

    def smooth(lap, later):
        t = count - 1 - lap
        means = xs[t, :, columns]
        priors = ps[t, :, columns]
        gains = g_all[t]
        rows = []
        for k in reversed(range(steps)):
            later = means[k : k + 1] + gains[k : k + 1] * (later - priors[k : k + 1])
            rows.insert(0, later)

        @pl.when(t == me)
        def _():
            out_ref[0] = means
            for k in range(steps):
                out_ref[1, k : k + 1, :] = rows[k]

        return later

    lax.fori_loop(0, count - me, smooth, ps[count - 1, steps - 1 : steps, columns])

    @pl.loop(1, count)
    def _(d):
        for i in (0, 1):
            send(i, lax.rem(me + d, count)).wait_send()

    @pl.loop(0, me)
    def _(peer):
        send(2, peer).wait_send()


def shares(width):
    return tuple(matrix_part(width, eighths) for eighths in SHARES)


def parted(both_ref, mean_ref, rec_ref):
    mean_ref[...] = both_ref[0]
    rec_ref[...] = both_ref[1]


def body(z, mask, f, h, mw, gain, x0):
    count = lax.axis_size("tm")
    steps, measures = z.shape
    width = f.shape[0]
    own = gain.shape[1]
    vmem = pl.BlockSpec(memory_space=pltpu.VMEM)
    hbm = pl.BlockSpec(memory_space=pltpu.HBM)
    out = jax.ShapeDtypeStruct((steps, own), jnp.float32)
    half = jnp.bfloat16
    f_part, u_part = shares(width)
    both = pl.pallas_call(
        kernel,
        out_shape=jax.ShapeDtypeStruct((2, steps, own), jnp.float32),
        in_specs=[hbm] * 7,
        out_specs=vmem,
        scratch_shapes=[
            pltpu.VMEM((1, measures), jnp.float32),
            pltpu.VMEM((1, width), jnp.float32),
            pltpu.VMEM((count, steps, measures), jnp.float32),
            pltpu.VMEM((count, steps, measures), jnp.int32),
            pltpu.VMEM((count, steps, own), jnp.float32),
            pltpu.VMEM((measures + width, width), jnp.float32),
            pltpu.VMEM((measures, width), jnp.float32),
            pltpu.VMEM((width, max(f_part, CHUNK)), half),
            pltpu.VMEM((width, max(f_part, CHUNK)), half),
            pltpu.VMEM((measures, max(u_part, CHUNK)), half),
            pltpu.VMEM((measures, max(u_part, CHUNK)), half),
            pltpu.VMEM((width - u_part, measures), jnp.float32),
            pltpu.VMEM((count, steps, width), jnp.float32),
            pltpu.VMEM((count, steps, width), jnp.float32),
            pltpu.SemaphoreType.DMA((3, count)),
            pltpu.SemaphoreType.DMA((3, count)),
            pltpu.SemaphoreType.DMA(((width + measures) // CHUNK,)),
            pltpu.SemaphoreType.DMA((5,)),
        ],
        compiler_params=pltpu.CompilerParams(
            collective_id=0, has_side_effects=True, vmem_limit_bytes=60 * 2**20
        ),
    )(z, mask, f, h, mw.reshape(1, -1), gain, x0.reshape(1, -1))
    return pl.pallas_call(
        parted, out_shape=(out, out), in_specs=[vmem], out_specs=(vmem, vmem)
    )(both)


def solution(mesh):
    placed = (P("tm", None), P("tm", None), P(), P(), P(), P("tm", "rows"), P())
    return jax.shard_map(
        body,
        mesh=mesh,
        in_specs=placed,
        out_specs=(P("tm", "rows"), P("tm", "rows")),
        check_vma=False,
    )
```

```python
import functools

import jax
import jax.numpy as jnp
from jax import lax
from jax.experimental import pallas as pl
from jax.experimental.pallas import tpu as pltpu
from jax.sharding import PartitionSpec as P

MESH = pl.DeviceIdType.MESH
CHUNK = 128
BAND = 256
PUSH_AT = 2
SHARES = (4, 1)


def turned(rows, by):
    return pltpu.roll(rows, by, 0)


def split_rows(rows):
    high = rows.astype(jnp.bfloat16).astype(jnp.float32)
    even = lax.broadcasted_iota(jnp.int32, rows.shape, 0) % 2 == 0
    return jnp.where(even, high, rows - high).astype(jnp.bfloat16)


def apply(rows, plain, firsts, high, low):
    depth = plain.shape[1]
    if high is not None:
        left = split_rows(rows)
        upper = jnp.dot(left, high[...], preferred_element_type=jnp.float32)
        lower = jnp.dot(left, low[...], preferred_element_type=jnp.float32)
    parts = []
    for first in firsts:
        sums = None
        for at in range(0, depth, CHUNK):
            block = plain[first : first + CHUNK, at : at + CHUNK].reshape(CHUNK // 8, 8, CHUNK)
            term = block * rows[None, :, at : at + CHUNK]
            sums = term if sums is None else sums + term
        part = jnp.sum(sums.reshape(CHUNK, CHUNK).T.reshape(CHUNK // 8, 8, CHUNK), axis=0)
        for by in (4, 2, 1):
            part += turned(part, by)
        parts.append(part)
    if high is None:
        return parts, []
    total = upper + lower
    return parts, [total + turned(total, 1)]


def matrix_part(size, eighths):
    return size * eighths // 8 // CHUNK * CHUNK


def halves(value):
    high = value.astype(jnp.bfloat16)
    return high, (value - high.astype(jnp.float32)).astype(jnp.bfloat16)


def kernel(
    z_ref, m_ref, f_hbm, h_hbm, mw_hbm, g_ref, x0_hbm,
    out_ref,
    mw_ref, x0_ref, z_all, m_all, g_all, gf, h_in, ft_hi, ft_lo, h_hi, h_lo, ht_in, xs, ps,
    send_sem, recv_sem, load_sem, own_sem,
):
    me = lax.axis_index("tm")
    count = lax.axis_size("tm")
    steps = z_ref.shape[0]
    width = f_hbm.shape[0]
    measures = h_hbm.shape[0]
    own = g_ref.shape[1]
    f_chunks, h_chunks = width // CHUNK, measures // CHUNK

    def load(c):
        if c < h_chunks:
            rows = pl.ds(c * CHUNK, CHUNK)
            return pltpu.make_async_copy(h_hbm.at[rows], h_in.at[rows], load_sem.at[c])
        rows = pl.ds((c - h_chunks) * CHUNK, CHUNK)
        target = gf.at[pl.ds(measures + (c - h_chunks) * CHUNK, CHUNK)]
        return pltpu.make_async_copy(f_hbm.at[rows], target, load_sem.at[c])

    barrier = pltpu.get_barrier_semaphore()

    @pl.loop(1, count)
    def _(d):
        peer = lax.rem(me + d, count)
        pl.semaphore_signal(barrier, inc=1, device_id={"tm": peer}, device_id_type=MESH)

    pairs = ((z_ref, z_all), (m_ref, m_all), (g_ref, g_all))
    loads = [(source, target.at[me]) for source, target in pairs] + [(mw_hbm, mw_ref), (x0_hbm, x0_ref)]
    own_loads = [pltpu.make_async_copy(*ends, own_sem.at[n]) for n, ends in enumerate(loads)]
    early = h_chunks + BAND // CHUNK
    for c in range(early):
        load(c).start()
    for copy in own_loads:
        copy.start()
    for copy in own_loads:
        copy.wait()

    def send(i, peer):
        return pltpu.make_async_remote_copy(
            src_ref=pairs[i][0], dst_ref=pairs[i][1].at[me],
            send_sem=send_sem.at[i, peer], recv_sem=recv_sem.at[i, me],
            device_id={"tm": peer}, device_id_type=MESH,
        )

    def arrival(i, t):
        return pltpu.make_async_remote_copy(
            src_ref=pairs[i][0], dst_ref=pairs[i][1].at[t],
            send_sem=send_sem.at[i, 0], recv_sem=recv_sem.at[i, t],
            device_id={"tm": lax.rem(me + 1, count)}, device_id_type=MESH,
        )

    def push():
        pl.semaphore_wait(barrier, count - 1)

        @pl.loop(1, count)
        def _(d):
            peer = lax.rem(me + d, count)
            for i in (0, 1):
                send(i, peer).start()

        @pl.loop(0, me)
        def _(peer):
            send(2, peer).start()

    f_part, u_part = shares(width)
    u_plain = width - u_part
    for c in range(h_chunks):
        load(c).wait()
    edges = [*range(0, PUSH_AT * BAND + 1, BAND), width]
    for b, (low_edge, high_edge) in enumerate(zip(edges, edges[1:])):
        if b == PUSH_AT:
            push()
        for c in range(low_edge // CHUNK, high_edge // CHUNK):
            load(h_chunks + c).wait()
        if b == 0:
            for c in range(early, f_chunks + h_chunks):
                load(c).start()
        high, low = halves(gf[measures + low_edge : measures + high_edge, :])
        h_high, h_low = halves(h_in[:, low_edge:high_edge])
        term = jnp.dot(
            jnp.concatenate([h_high, h_low, h_high], axis=1),
            jnp.concatenate([high, high, low], axis=0),
            preferred_element_type=jnp.float32,
        )
        gf[:measures, :] = term if b == 0 else gf[:measures, :] + term
        if b == 0:
            ht_in[...] = h_in[:, :u_plain].T
            if u_part:
                h_hi[...], h_lo[...] = halves(h_in[:, u_plain:])
        for first in range(low_edge, min(high_edge, f_part), CHUNK):
            to = pl.ds(first, CHUNK)
            ft_hi[:, to], ft_lo[:, to] = halves(gf[measures + first : measures + first + CHUNK, :].T)

    def start(state):
        parts, _ = apply(state, gf, range(measures, measures + width, CHUNK), None, None)
        predicted = jnp.concatenate(parts, axis=1)
        parts, _ = apply(predicted, h_in, range(0, measures, CHUNK), None, None)
        return predicted, jnp.concatenate(parts, axis=1)

    def advance(state):
        firsts = [*range(0, measures, CHUNK), *range(measures + f_part, measures + width, CHUNK)]
        parts, shared = apply(state, gf, firsts, *((ft_hi, ft_lo) if f_part else (None, None)))
        seen = jnp.concatenate(parts[: measures // CHUNK], axis=1)
        return jnp.concatenate([*shared, *parts[measures // CHUNK :]], axis=1), seen

    def spread(change):
        parts, shared = apply(
            change, ht_in, range(0, u_plain, CHUNK), *((h_hi, h_lo) if u_part else (None, None))
        )
        return jnp.concatenate([*parts, *shared], axis=1)

    def block_of_steps(t, carried):
        predicted, seen = carried

        @pl.when(t != me)
        def _():
            arrival(0, t).wait_recv()
            arrival(1, t).wait_recv()

        weights = m_all[t].astype(jnp.float32) * mw_ref[...]
        readings = z_all[t]
        alike = functools.partial(jnp.broadcast_to, shape=(8, measures))
        for k in range(steps):
            change = alike(weights[k : k + 1]) * (alike(readings[k : k + 1]) - seen)
            state = predicted + spread(change)
            predicted, seen = advance(state)
            xs[t, k : k + 1, :] = state[:1]
            ps[t, k : k + 1, :] = predicted[:1]
        return predicted, seen

    lax.fori_loop(0, count, block_of_steps, start(jnp.broadcast_to(x0_ref[...], (8, width))))

    columns = pl.ds(pl.multiple_of(lax.axis_index("rows") * own, own), own)

    @pl.loop(me + 1, count)
    def _(t):
        arrival(2, t).wait_recv()

    def smooth(lap, later):
        t = count - 1 - lap
        means = xs[t, :, columns]
        priors = ps[t, :, columns]
        gains = g_all[t]
        rows = []
        for k in reversed(range(steps)):
            later = means[k : k + 1] + gains[k : k + 1] * (later - priors[k : k + 1])
            rows.insert(0, later)

        @pl.when(t == me)
        def _():
            out_ref[0] = means
            for k in range(steps):
                out_ref[1, k : k + 1, :] = rows[k]

        return later

    lax.fori_loop(0, count - me, smooth, ps[count - 1, steps - 1 : steps, columns])

    @pl.loop(1, count)
    def _(d):
        for i in (0, 1):
            send(i, lax.rem(me + d, count)).wait_send()

    @pl.loop(0, me)
    def _(peer):
        send(2, peer).wait_send()


def shares(width):
    return tuple(matrix_part(width, eighths) for eighths in SHARES)


def parted(both_ref, mean_ref, rec_ref):
    mean_ref[...] = both_ref[0]
    rec_ref[...] = both_ref[1]


def body(z, mask, f, h, mw, gain, x0):
    count = lax.axis_size("tm")
    steps, measures = z.shape
    width = f.shape[0]
    own = gain.shape[1]
    vmem = pl.BlockSpec(memory_space=pltpu.VMEM)
    hbm = pl.BlockSpec(memory_space=pltpu.HBM)
    out = jax.ShapeDtypeStruct((steps, own), jnp.float32)
    half = jnp.bfloat16
    f_part, u_part = shares(width)
    both = pl.pallas_call(
        kernel,
        out_shape=jax.ShapeDtypeStruct((2, steps, own), jnp.float32),
        in_specs=[hbm] * 7,
        out_specs=vmem,
        scratch_shapes=[
            pltpu.VMEM((1, measures), jnp.float32),
            pltpu.VMEM((1, width), jnp.float32),
            pltpu.VMEM((count, steps, measures), jnp.float32),
            pltpu.VMEM((count, steps, measures), jnp.int32),
            pltpu.VMEM((count, steps, own), jnp.float32),
            pltpu.VMEM((measures + width, width), jnp.float32),
            pltpu.VMEM((measures, width), jnp.float32),
            pltpu.VMEM((width, max(f_part, CHUNK)), half),
            pltpu.VMEM((width, max(f_part, CHUNK)), half),
            pltpu.VMEM((measures, max(u_part, CHUNK)), half),
            pltpu.VMEM((measures, max(u_part, CHUNK)), half),
            pltpu.VMEM((width - u_part, measures), jnp.float32),
            pltpu.VMEM((count, steps, width), jnp.float32),
            pltpu.VMEM((count, steps, width), jnp.float32),
            pltpu.SemaphoreType.DMA((3, count)),
            pltpu.SemaphoreType.DMA((3, count)),
            pltpu.SemaphoreType.DMA(((width + measures) // CHUNK,)),
            pltpu.SemaphoreType.DMA((5,)),
        ],
        compiler_params=pltpu.CompilerParams(
            collective_id=0, has_side_effects=True, vmem_limit_bytes=60 * 2**20
        ),
    )(z, mask, f, h, mw.reshape(1, -1), gain, x0.reshape(1, -1))
    return pl.pallas_call(
        parted, out_shape=(out, out), in_specs=[vmem], out_specs=(vmem, vmem)
    )(both)


def solution(mesh):
    placed = (P("tm", None), P("tm", None), P(), P(), P(), P("tm", "rows"), P())
    return jax.shard_map(
        body,
        mesh=mesh,
        in_specs=placed,
        out_specs=(P("tm", "rows"), P("tm", "rows")),
        check_vma=False,
    )
```

```python
import functools

import jax
import jax.numpy as jnp
from jax import lax
from jax.experimental import pallas as pl
from jax.experimental.pallas import tpu as pltpu
from jax.sharding import PartitionSpec as P

MESH = pl.DeviceIdType.MESH
CHUNK = 128
BAND = 256
PUSH_AT = 2
SHARES = (4, 2)


def turned(rows, by):
    return pltpu.roll(rows, by, 0)


def split_rows(rows):
    high = rows.astype(jnp.bfloat16).astype(jnp.float32)
    even = lax.broadcasted_iota(jnp.int32, rows.shape, 0) % 2 == 0
    return jnp.where(even, high, rows - high).astype(jnp.bfloat16)


def apply(rows, plain, firsts, high, low):
    depth = plain.shape[1]
    if high is not None:
        left = split_rows(rows)
        upper = jnp.dot(left, high[...], preferred_element_type=jnp.float32)
        lower = jnp.dot(left, low[...], preferred_element_type=jnp.float32)
    parts = []
    for first in firsts:
        sums = None
        for at in range(0, depth, CHUNK):
            block = plain[first : first + CHUNK, at : at + CHUNK].reshape(CHUNK // 8, 8, CHUNK)
            term = block * rows[None, :, at : at + CHUNK]
            sums = term if sums is None else sums + term
        part = jnp.sum(sums.reshape(CHUNK, CHUNK).T.reshape(CHUNK // 8, 8, CHUNK), axis=0)
        for by in (4, 2, 1):
            part += turned(part, by)
        parts.append(part)
    if high is None:
        return parts, []
    total = upper + lower
    return parts, [total + turned(total, 1)]


def matrix_part(size, eighths):
    return size * eighths // 8 // CHUNK * CHUNK


def halves(value):
    high = value.astype(jnp.bfloat16)
    return high, (value - high.astype(jnp.float32)).astype(jnp.bfloat16)


def kernel(
    z_ref, m_ref, f_hbm, h_hbm, mw_hbm, g_ref, x0_hbm,
    out_ref,
    mw_ref, x0_ref, z_all, m_all, g_all, gf, h_in, ft_hi, ft_lo, h_hi, h_lo, ht_in, xs, ps,
    send_sem, recv_sem, load_sem, own_sem,
):
    me = lax.axis_index("tm")
    count = lax.axis_size("tm")
    steps = z_ref.shape[0]
    width = f_hbm.shape[0]
    measures = h_hbm.shape[0]
    own = g_ref.shape[1]
    f_chunks, h_chunks = width // CHUNK, measures // CHUNK

    def load(c):
        if c < h_chunks:
            rows = pl.ds(c * CHUNK, CHUNK)
            return pltpu.make_async_copy(h_hbm.at[rows], h_in.at[rows], load_sem.at[c])
        rows = pl.ds((c - h_chunks) * CHUNK, CHUNK)
        target = gf.at[pl.ds(measures + (c - h_chunks) * CHUNK, CHUNK)]
        return pltpu.make_async_copy(f_hbm.at[rows], target, load_sem.at[c])

    barrier = pltpu.get_barrier_semaphore()

    @pl.loop(1, count)
    def _(d):
        peer = lax.rem(me + d, count)
        pl.semaphore_signal(barrier, inc=1, device_id={"tm": peer}, device_id_type=MESH)

    pairs = ((z_ref, z_all), (m_ref, m_all), (g_ref, g_all))
    loads = [(source, target.at[me]) for source, target in pairs] + [(mw_hbm, mw_ref), (x0_hbm, x0_ref)]
    own_loads = [pltpu.make_async_copy(*ends, own_sem.at[n]) for n, ends in enumerate(loads)]
    early = h_chunks + BAND // CHUNK
    for c in range(early):
        load(c).start()
    for copy in own_loads:
        copy.start()
    for copy in own_loads:
        copy.wait()

    def send(i, peer):
        return pltpu.make_async_remote_copy(
            src_ref=pairs[i][0], dst_ref=pairs[i][1].at[me],
            send_sem=send_sem.at[i, peer], recv_sem=recv_sem.at[i, me],
            device_id={"tm": peer}, device_id_type=MESH,
        )

    def arrival(i, t):
        return pltpu.make_async_remote_copy(
            src_ref=pairs[i][0], dst_ref=pairs[i][1].at[t],
            send_sem=send_sem.at[i, 0], recv_sem=recv_sem.at[i, t],
            device_id={"tm": lax.rem(me + 1, count)}, device_id_type=MESH,
        )

    def push():
        pl.semaphore_wait(barrier, count - 1)

        @pl.loop(1, count)
        def _(d):
            peer = lax.rem(me + d, count)
            for i in (0, 1):
                send(i, peer).start()

        @pl.loop(0, me)
        def _(peer):
            send(2, peer).start()

    f_part, u_part = shares(width)
    u_plain = width - u_part
    for c in range(h_chunks):
        load(c).wait()
    edges = [*range(0, PUSH_AT * BAND + 1, BAND), width]
    for b, (low_edge, high_edge) in enumerate(zip(edges, edges[1:])):
        if b == PUSH_AT:
            push()
        for c in range(low_edge // CHUNK, high_edge // CHUNK):
            load(h_chunks + c).wait()
        if b == 0:
            for c in range(early, f_chunks + h_chunks):
                load(c).start()
        high, low = halves(gf[measures + low_edge : measures + high_edge, :])
        h_high, h_low = halves(h_in[:, low_edge:high_edge])
        term = jnp.dot(
            jnp.concatenate([h_high, h_low, h_high], axis=1),
            jnp.concatenate([high, high, low], axis=0),
            preferred_element_type=jnp.float32,
        )
        gf[:measures, :] = term if b == 0 else gf[:measures, :] + term
        if b == 0:
            ht_in[...] = h_in[:, :u_plain].T
            if u_part:
                h_hi[...], h_lo[...] = halves(h_in[:, u_plain:])
        for first in range(low_edge, min(high_edge, f_part), CHUNK):
            to = pl.ds(first, CHUNK)
            ft_hi[:, to], ft_lo[:, to] = halves(gf[measures + first : measures + first + CHUNK, :].T)

    def start(state):
        parts, _ = apply(state, gf, range(measures, measures + width, CHUNK), None, None)
        predicted = jnp.concatenate(parts, axis=1)
        parts, _ = apply(predicted, h_in, range(0, measures, CHUNK), None, None)
        return predicted, jnp.concatenate(parts, axis=1)

    def advance(state):
        firsts = [*range(0, measures, CHUNK), *range(measures + f_part, measures + width, CHUNK)]
        parts, shared = apply(state, gf, firsts, *((ft_hi, ft_lo) if f_part else (None, None)))
        seen = jnp.concatenate(parts[: measures // CHUNK], axis=1)
        return jnp.concatenate([*shared, *parts[measures // CHUNK :]], axis=1), seen

    def spread(change):
        parts, shared = apply(
            change, ht_in, range(0, u_plain, CHUNK), *((h_hi, h_lo) if u_part else (None, None))
        )
        return jnp.concatenate([*parts, *shared], axis=1)

    def block_of_steps(t, carried):
        predicted, seen = carried

        @pl.when(t != me)
        def _():
            arrival(0, t).wait_recv()
            arrival(1, t).wait_recv()

        weights = m_all[t].astype(jnp.float32) * mw_ref[...]
        readings = z_all[t]
        alike = functools.partial(jnp.broadcast_to, shape=(8, measures))
        for k in range(steps):
            change = alike(weights[k : k + 1]) * (alike(readings[k : k + 1]) - seen)
            state = predicted + spread(change)
            predicted, seen = advance(state)
            xs[t, k : k + 1, :] = state[:1]
            ps[t, k : k + 1, :] = predicted[:1]
        return predicted, seen

    lax.fori_loop(0, count, block_of_steps, start(jnp.broadcast_to(x0_ref[...], (8, width))))

    columns = pl.ds(pl.multiple_of(lax.axis_index("rows") * own, own), own)

    @pl.loop(me + 1, count)
    def _(t):
        arrival(2, t).wait_recv()

    def smooth(lap, later):
        t = count - 1 - lap
        means = xs[t, :, columns]
        priors = ps[t, :, columns]
        gains = g_all[t]
        rows = []
        for k in reversed(range(steps)):
            later = means[k : k + 1] + gains[k : k + 1] * (later - priors[k : k + 1])
            rows.insert(0, later)

        @pl.when(t == me)
        def _():
            out_ref[0] = means
            for k in range(steps):
                out_ref[1, k : k + 1, :] = rows[k]

        return later

    lax.fori_loop(0, count - me, smooth, ps[count - 1, steps - 1 : steps, columns])

    @pl.loop(1, count)
    def _(d):
        for i in (0, 1):
            send(i, lax.rem(me + d, count)).wait_send()

    @pl.loop(0, me)
    def _(peer):
        send(2, peer).wait_send()


def shares(width):
    return tuple(matrix_part(width, eighths) for eighths in SHARES)


def parted(both_ref, mean_ref, rec_ref):
    mean_ref[...] = both_ref[0]
    rec_ref[...] = both_ref[1]


def body(z, mask, f, h, mw, gain, x0):
    count = lax.axis_size("tm")
    steps, measures = z.shape
    width = f.shape[0]
    own = gain.shape[1]
    vmem = pl.BlockSpec(memory_space=pltpu.VMEM)
    hbm = pl.BlockSpec(memory_space=pltpu.HBM)
    out = jax.ShapeDtypeStruct((steps, own), jnp.float32)
    half = jnp.bfloat16
    f_part, u_part = shares(width)
    both = pl.pallas_call(
        kernel,
        out_shape=jax.ShapeDtypeStruct((2, steps, own), jnp.float32),
        in_specs=[hbm] * 7,
        out_specs=vmem,
        scratch_shapes=[
            pltpu.VMEM((1, measures), jnp.float32),
            pltpu.VMEM((1, width), jnp.float32),
            pltpu.VMEM((count, steps, measures), jnp.float32),
            pltpu.VMEM((count, steps, measures), jnp.int32),
            pltpu.VMEM((count, steps, own), jnp.float32),
            pltpu.VMEM((measures + width, width), jnp.float32),
            pltpu.VMEM((measures, width), jnp.float32),
            pltpu.VMEM((width, max(f_part, CHUNK)), half),
            pltpu.VMEM((width, max(f_part, CHUNK)), half),
            pltpu.VMEM((measures, max(u_part, CHUNK)), half),
            pltpu.VMEM((measures, max(u_part, CHUNK)), half),
            pltpu.VMEM((width - u_part, measures), jnp.float32),
            pltpu.VMEM((count, steps, width), jnp.float32),
            pltpu.VMEM((count, steps, width), jnp.float32),
            pltpu.SemaphoreType.DMA((3, count)),
            pltpu.SemaphoreType.DMA((3, count)),
            pltpu.SemaphoreType.DMA(((width + measures) // CHUNK,)),
            pltpu.SemaphoreType.DMA((5,)),
        ],
        compiler_params=pltpu.CompilerParams(
            collective_id=0, has_side_effects=True, vmem_limit_bytes=60 * 2**20
        ),
    )(z, mask, f, h, mw.reshape(1, -1), gain, x0.reshape(1, -1))
    return pl.pallas_call(
        parted, out_shape=(out, out), in_specs=[vmem], out_specs=(vmem, vmem)
    )(both)


def solution(mesh):
    placed = (P("tm", None), P("tm", None), P(), P(), P(), P("tm", "rows"), P())
    return jax.shard_map(
        body,
        mesh=mesh,
        in_specs=placed,
        out_specs=(P("tm", "rows"), P("tm", "rows")),
        check_vma=False,
    )
```
